32 devices in a mesh: gx: 8 (over z, y), gy: 4 (over x, core).
Axes of the slice: x: 2, y: 2, z: 4, core: 2. Of those that a mesh axis runs over, the one named last changes fastest.
Arguments:
- charges: float32 [256, 128, 256], P('gx', 'gy'), may hold values from -6 to 6
- kernel_taps: float32 [3, 3, 21], replicated, may hold values from -1.08 to 1.08
Outputs:
- potential: float32 [256, 128, 256], P('gx', 'gy')
The draws below stay inside these ranges and needn't reach their ends.
All inputs are finite; a program needn't handle non-finite values.
Results may differ from the reference program's by a relative error of at most 0.035.
Values sent between devices are 32-bit elements; how exact they have to be, the bound alone decides.
A program may use at most 128 MiB of HBM per device.

```python
import jax
import jax.numpy as jnp
from jax import lax

NZ = 256
TERMS = 3
LEVELS = 3
NX = 256
NY = 128
TAPS = 21


def shard_levels(key, shape, pieces, least, high):
    factor_of = 1.0
    for position, shards_of in pieces:
        heights = jax.random.uniform(jax.random.fold_in(jax.random.fold_in(key, 6), position), (shards_of,), jnp.float32, least / len(pieces), high / len(pieces))
        factor_of = factor_of * jnp.repeat(jnp.exp(heights), shape[position] // shards_of).reshape((-1,) + (1,) * (len(shape) - 1 - position))
    return factor_of


def bell_draw(key, dims, scale, bound, cuts=(), held_as=jnp.bfloat16):
    values = scale * jax.random.normal(key, dims, jnp.float32)
    if cuts:
        values = values * shard_levels(key, dims, cuts, -0.22, 0.18)
    return jnp.clip(values, -bound, bound).astype(held_as)


def setup_inputs(seed: int = 0) -> dict:
    key_of = jax.random.split(jax.random.key(seed), 3)
    charges = bell_draw(key_of[0], (NX, NY, NZ), 1.0, 6.0, ((0, 8), (1, 4)), jnp.float32)
    kernel_taps = bell_draw(key_of[1], (LEVELS, TERMS, TAPS), 0.18, 1.08, (), jnp.float32)
    return dict(charges=charges, kernel_taps=kernel_taps)


SPLINE = (0.125, 0.5, 0.75, 0.5, 0.125)


def correlate(values, taps, along):
    length = values.shape[along]
    tap_count = taps.shape[0]
    radius = tap_count // 2
    wrapped = (jnp.arange(tap_count, dtype=jnp.int32) - radius) % length
    onehot = (wrapped[:, None] == jnp.arange(length, dtype=jnp.int32)[None, :]).astype(jnp.float32)
    profile = jnp.dot(taps, onehot, preferred_element_type=jnp.float32, precision=lax.Precision.HIGHEST)
    shaped = [1] * values.ndim
    shaped[along] = -1
    spectrum = jnp.fft.rfft(values, axis=along) * jnp.conj(jnp.fft.rfft(profile)).reshape(shaped)
    return jnp.fft.irfft(spectrum, n=length, axis=along)


def convolve(values, taps):
    summed = jnp.zeros(values.shape, jnp.float32)
    for member in range(taps.shape[0]):
        sectioned = correlate(values, taps[member], 0)
        sectioned = correlate(sectioned, taps[member], 1)
        summed = summed + correlate(sectioned, taps[member], 2)
    return summed


def restrict(values, along):
    length = values.shape[along]
    summed = jnp.zeros(values.shape, jnp.float32)
    for shift_by in range(-2, 3):
        summed = summed + SPLINE[shift_by + 2] * jnp.roll(values, -shift_by, along)
    return lax.slice_in_dim(summed, 0, length, 2, along)


def prolong(values, along):
    blank = jnp.zeros(values.shape, jnp.float32)
    shaped = list(values.shape)
    shaped[along] = 2 * shaped[along]
    spread = jnp.stack([values, blank], axis=along + 1).reshape(shaped)
    summed = jnp.zeros(spread.shape, jnp.float32)
    for shift_by in range(-2, 3):
        summed = summed + SPLINE[shift_by + 2] * jnp.roll(spread, shift_by, along)
    return summed


def restrict_grid(values):
    return restrict(restrict(restrict(values, 0), 1), 2)


def prolong_grid(values):
    return prolong(prolong(prolong(values, 0), 1), 2)


def reference(charges, kernel_taps):
    coarse = restrict_grid(charges)
    summit = restrict_grid(coarse)
    top_field = convolve(summit, kernel_taps[2])
    middle = convolve(coarse, kernel_taps[1]) + prolong_grid(top_field)
    return convolve(charges, kernel_taps[0]) + prolong_grid(middle)
```

```python
import jax
import jax.numpy as jnp
from jax import lax
from jax.sharding import PartitionSpec as P

SPLINE = (0.125, 0.5, 0.75, 0.5, 0.125)


def padded_2(x, sides, width):
    for axis, dim in sides:
        peers, length = (lax.axis_size(axis), x.shape[dim])
        up = [(i, (i + 1) % peers) for i in range(peers)]
        down = [(j, i) for i, j in up]
        last = lax.slice_in_dim(x, length - width, length, axis=dim)
        first = lax.slice_in_dim(x, 0, width, axis=dim)
        before = lax.ppermute(last, axis, up)
        after = lax.ppermute(first, axis, down)
        x = jnp.concatenate([before, x, after], axis=dim)
    return x


def contract(formula, left, right):
    return jnp.einsum(formula, left, right, precision=lax.Precision.HIGH)


def grid_ids(count_rows, count_cols):
    row_ids = lax.broadcasted_iota(jnp.int32, (count_rows, count_cols), 0)
    col_ids = lax.broadcasted_iota(jnp.int32, (count_rows, count_cols), 1)
    return (row_ids, col_ids)


def spline_table(offsets):
    table = jnp.zeros(offsets.shape, jnp.float32)
    for position in range(5):
        table = table + SPLINE[position] * (offsets == position).astype(jnp.float32)
    return table


def spread_taps(taps, offsets):
    table = jnp.zeros((taps.shape[0],) + offsets.shape, jnp.float32)
    for position in range(taps.shape[1]):
        table = table + jnp.where(offsets == position, taps[:, position, None, None], 0.0)
    return table


def band_taps(taps, count_rows, count_cols):
    row_ids, col_ids = grid_ids(count_rows, count_cols)
    return spread_taps(taps, col_ids - row_ids)


def cycle_taps(taps, length):
    row_ids, col_ids = grid_ids(length, length)
    tap_count = taps.shape[1]
    shift = (col_ids - row_ids + tap_count // 2) % length
    table = spread_taps(taps, shift)
    for lap in range(1, -(-tap_count // length)):
        table = table + spread_taps(taps, shift + lap * length)
    return table


def restrict_band(count_rows, count_cols, margin):
    row_ids, col_ids = grid_ids(count_rows, count_cols)
    return spline_table(col_ids - margin - 2 * row_ids + 2)


def restrict_cycle(length):
    row_ids, col_ids = grid_ids(length // 2, length)
    return spline_table((col_ids - 2 * row_ids + 2) % length)


def prolong_band(count_rows, count_cols):
    row_ids, col_ids = grid_ids(count_rows, count_cols)
    return spline_table(row_ids - 2 * col_ids + 4)


def prolong_cycle(count_rows, coarse_len, offset):
    row_ids, col_ids = grid_ids(count_rows, coarse_len)
    return spline_table((offset + row_ids - 2 * col_ids + 2) % (2 * coarse_len))


def body(charges, kernel_taps):
    radius = kernel_taps.shape[2] // 2
    margin = radius + 1
    term_count = kernel_taps.shape[1]
    rows_x, rows_y, cells_z = charges.shape
    half_x, half_y, half_z = (rows_x // 2, rows_y // 2, cells_z // 2)
    quarter_x, quarter_z = (rows_x // 4, cells_z // 4)
    count_x = lax.axis_size("gx")
    count_y = lax.axis_size("gy")
    wide_y = rows_y * count_y
    quarter_y = wide_y // 4
    taps_fine, taps_middle, taps_top = (kernel_taps[0], kernel_taps[1], kernel_taps[2])
    padded = padded_2(charges, (("gx", 0), ("gy", 1)), radius)
    across_x = band_taps(taps_fine, rows_x, rows_x + 2 * radius)
    across_y = band_taps(taps_fine, rows_y, rows_y + 2 * radius)
    across_z = cycle_taps(taps_fine, cells_z)
    direct_fine = jnp.zeros(charges.shape, jnp.float32)
    for member in range(term_count):
        sectioned = contract("mc,cyz->myz", across_x[member], padded)
        sectioned = contract("nc,mcz->mnz", across_y[member], sectioned)
        direct_fine = direct_fine + contract("mnz,wz->mnw", sectioned, across_z[member])
    coarse = contract("mc,cyz->myz", restrict_band(half_x, rows_x + 2 * radius, radius), padded)
    coarse = contract("nc,mcz->mnz", restrict_band(half_y, rows_y + 2 * radius, radius), coarse)
    coarse = contract("mnz,wz->mnw", coarse, restrict_cycle(cells_z))
    middle_x = band_taps(taps_middle, half_x + 2, half_x + 2 * margin)
    middle_z = cycle_taps(taps_middle, half_z)
    down_x = restrict_band(quarter_x, half_x + 2 * margin, margin)
    down_z = restrict_cycle(half_z)
    up_z = prolong_cycle(half_z, quarter_z, 0)
    rimmed = padded_2(coarse, (("gx", 0), ("gy", 1)), margin)
    middle_y = band_taps(taps_middle, half_y + 2, half_y + 2 * margin)
    direct_middle = jnp.zeros((half_x + 2, half_y + 2, half_z), jnp.float32)
    for member in range(term_count):
        sectioned = contract("mc,cyz->myz", middle_x[member], rimmed)
        sectioned = contract("nc,mcz->mnz", middle_y[member], sectioned)
        direct_middle = direct_middle + contract("mnz,wz->mnw", sectioned, middle_z[member])
    summit = contract("mc,cyz->myz", down_x, rimmed)
    summit = contract(
        "nc,mcz->mnz", restrict_band(half_y // 2, half_y + 2 * margin, margin), summit
    )
    summit = contract("mnz,wz->mnw", summit, down_z)
    lift_y = prolong_cycle(half_y + 2, quarter_y, lax.axis_index("gy") * half_y - 1)
    spread_y = prolong_band(rows_y, half_y + 2)
    top_y = cycle_taps(taps_top, quarter_y)
    top_z = cycle_taps(taps_top, quarter_z)
    full_x = quarter_x * count_x
    top_x = cycle_taps(taps_top, full_x)
    along_z = jnp.stack(
        [contract("mnz,wz->mnw", summit, top_z[member]) for member in range(term_count)]
    )
    portion = lax.all_to_all(along_z, "gy", split_axis=3, concat_axis=2, tiled=True)
    turned_yz = jnp.stack(
        [contract("nc,mcw->mnw", top_y[member], portion[member]) for member in range(term_count)]
    )
    up_x = prolong_cycle(2 * full_x, full_x, 0)
    portion = lax.all_to_all(turned_yz, "gx", split_axis=2, concat_axis=1, tiled=True)
    result = jnp.zeros(portion.shape[1:], jnp.float32)
    for member in range(term_count):
        result = result + contract("mc,cnw->mnw", top_x[member], portion[member])
    refined = contract("jm,mnw->jnw", up_x, result)
    rest_shape = refined.shape[1:]
    blocks = refined.reshape((count_x, half_x) + rest_shape)
    leading = jnp.roll(refined, 1, 0).reshape((count_x, half_x) + rest_shape)[:, :1]
    trailing = jnp.roll(refined, -1, 0).reshape((count_x, half_x) + rest_shape)[:, -1:]
    windows = jnp.concatenate([leading, blocks, trailing], axis=1)
    back_rows = lax.all_to_all(windows, "gx", split_axis=0, concat_axis=2, tiled=True)[0]
    returned = lax.all_gather(back_rows, "gy", axis=2, tiled=True)
    lifted = contract("jn,mnw->mjw", lift_y, returned)
    lifted = contract("mjz,wz->mjw", lifted, up_z)
    middle = direct_middle + lifted
    refined = contract("jm,myz->jyz", prolong_band(rows_x, half_x + 2), middle)
    refined = contract("jn,mnz->mjz", spread_y, refined)
    refined = contract("mjz,wz->mjw", refined, prolong_cycle(cells_z, half_z, 0))
    return direct_fine + refined


def solution(mesh):
    return jax.shard_map(
        body,
        mesh=mesh,
        in_specs=(P("gx", "gy", None), P()),
        out_specs=P("gx", "gy", None),
        check_vma=False,
    )
```

```python
import functools

import jax
import jax.numpy as jnp
import numpy as np
from jax import lax
from jax.experimental import pallas as pl
from jax.experimental.pallas import tpu as pltpu
from jax.sharding import PartitionSpec as P

SPLINE = (0.125, 0.5, 0.75, 0.5, 0.125)
F32, BF16 = jnp.float32, jnp.bfloat16
MESH = pl.DeviceIdType.MESH


def spline_at(offset):
    return SPLINE[offset + 2] if -2 <= offset <= 2 else 0.0


def fixed_table(rows, cols, width):
    table = np.zeros((width, len(cols)), np.float32)
    for a, fine in enumerate(rows):
        for b, other in enumerate(cols):
            if fine is not None and other is not None:
                table[a, b] = spline_at(other - 2 * fine)
    return table


def lifted_table(rows, cols, width):
    table = np.zeros((width, len(cols)), np.float32)
    for a, fine in enumerate(rows):
        for b, coarse in enumerate(cols):
            if coarse is not None:
                table[a, b] = spline_at(fine - 2 * coarse)
    return table


def twice(table):
    return jnp.asarray(np.concatenate([table, table], axis=1), BF16)


def halves(value):
    high = value.astype(BF16)
    return high, (value - high.astype(F32)).astype(BF16)


def dot(left, right):
    return jnp.dot(left, right, preferred_element_type=F32)


def stacked2(value):
    high, low = halves(value)
    return jnp.concatenate([high, low], axis=0)


def stacked3(value):
    high, low = halves(value)
    return jnp.concatenate([high, low, high], axis=0)


def repeat(count, step, body):
    def trip(i, carry):
        for k in range(step):
            body(i * step + k)
        return carry

    assert count % step == 0
    lax.fori_loop(0, count // step, trip, 0)


def kernel(nx, ny, radius, terms, taps, q, ry1, rz1, ry2, rz2, uy2, uz2, uy1, uz1, out,
           fine, mid, own2, line2, top, ty0, ty1, ty2, tz0, tz1, tz2,
           y0, s0, y1, s1, y2, s2, rx, r1, l1w, l2x, l2y, tx, ty, md, mx, my,
           send, recv):
    bx, by, bz = q.shape
    hx, hy, hz = bx // 2, by // 2, bz // 2
    ex, ey, ez = bx // 4, by // 4, bz // 4
    count = 2 * radius + 1
    margin = radius + 1
    me_x, me_y = lax.axis_index("gx"), lax.axis_index("gy")
    reach = 2
    wy = min(ny, 2 * reach + 1)
    low_y = -((wy - 1) // 2)

    def device(dx, dy):
        return {"gx": lax.rem(me_x + dx + nx, nx), "gy": lax.rem(me_y + dy + ny, ny)}

    peers = {}
    for dx, dy in [(a, b) for a in (-1, 0, 1) for b in (-1, 0, 1)] + [(-2, 0), (2, 0)] + [
        (0, -(low_y + k)) for k in range(wy)
    ]:
        if dx % nx or dy % ny:
            peers[(dx % nx, dy % ny)] = (dx, dy)
    barrier = pltpu.get_barrier_semaphore()
    for dx, dy in peers.values():
        pl.semaphore_signal(barrier, inc=1, device_id=device(dx, dy), device_id_type=MESH)

    def tap(level, member, position):
        return taps[(level * terms + member) * count + position]

    def band(level, member, rows, cols, first, cycle):
        offsets = (
            lax.broadcasted_iota(jnp.int32, (rows, cols), 1)
            - lax.broadcasted_iota(jnp.int32, (rows, cols), 0)
            + first
        )
        if cycle:
            offsets = jnp.where(offsets < 0, offsets + cycle, offsets)
            offsets = jnp.where(offsets >= cycle, offsets - cycle, offsets)
        table = jnp.zeros((rows, cols), F32)
        for position in range(count):
            table = jnp.where(offsets == position, tap(level, member, position), table)
        return table

    def y_table(ref, level, rows, cols, first, cycle):
        for member in range(terms):
            high, low = halves(band(level, member, rows, cols, first, cycle))
            at = slice(member * rows, (member + 1) * rows)
            ref[at, 0:cols] = high
            ref[at, cols : 2 * cols] = high
            ref[at, 2 * cols : 3 * cols] = low

    def z_table(ref, level, n):
        def rows_of(i):
            start = pl.multiple_of(i * 16, 16)
            offsets = (
                lax.broadcasted_iota(jnp.int32, (16, n), 0)
                + start
                - lax.broadcasted_iota(jnp.int32, (16, n), 1)
                + radius
            )
            offsets = jnp.where(offsets < 0, offsets + n, offsets)
            offsets = jnp.where(offsets >= n, offsets - n, offsets)
            for member in range(terms):
                table = jnp.zeros((16, n), F32)
                for position in range(count):
                    table = jnp.where(offsets == position, tap(level, member, position), table)
                high, low = halves(table)
                ref[member, 0, pl.ds(start, 16), :] = high
                ref[member, 1, pl.ds(start, 16), :] = low

        repeat(n // 16, 1, rows_of)

    sem = [0]

    def remote(source, target, dx, dy):
        index = sem[0]
        sem[0] += 1
        return pltpu.make_async_remote_copy(
            src_ref=source, dst_ref=target, send_sem=send.at[index], recv_sem=recv.at[index],
            device_id=device(dx, dy), device_id_type=MESH,
        )

    def both(copies):
        for copy in copies:
            copy.start()
        return copies

    def arrive(copies):
        for copy in copies:
            copy.wait_recv()

    pad = 2 * 8
    x0, x1, c0, c1 = radius, radius + bx, pad, pad + by
    back, ahead = 6, 3

    fine[x0:x1, c0:c1, :] = q[...]
    y_table(ty0, 0, by, by + 2 * pad, radius - pad, 0)
    pl.semaphore_wait(barrier, len(peers))
    near = []
    for dx, src_x, dst_x in ((1, (bx - back, bx), (x0 - back, x0)), (-1, (0, ahead), (x1, x1 + ahead)), (0, (0, bx), (x0, x1))):
        for dy, src_y, dst_y in ((1, (by - 8, by), (c0 - 8, c0)), (-1, (0, 8), (c1, c1 + 8)), (0, (0, by), (c0, c1))):
            if dx or dy:
                near.append(remote(q.at[slice(*src_x), slice(*src_y)], fine.at[slice(*dst_x), slice(*dst_y)], dx, dy))
    both(near)
    far = [
        remote(q.at[bx - radius : bx - back], fine.at[0 : x0 - back, c0:c1], 1, 0),
        remote(q.at[ahead:radius], fine.at[x1 + ahead : x1 + radius, c0:c1], -1, 0),
        remote(q.at[:, by - 16 : by - 8], fine.at[x0:x1, 0:8], 0, 1),
        remote(q.at[:, 8:16], fine.at[x0:x1, c1 + 8 : c1 + 16], 0, -1),
    ]
    y_table(ty1, 1, ty1.shape[0] // terms, hy + 2 * hy, radius - 1 * hy - (-1) , 0)
    y_table(ty2, 2, ty2.shape[0] // terms, wy * ey, low_y * ey + 1 + radius, wy * ey if ny <= 2 * reach + 1 else 0)
    z_table(tz0, 0, bz)
    z_table(tz1, 1, hz)
    z_table(tz2, 2, ez)
    arrive(near)

    rows1 = hx + 3
    base = x0 - back

    def restrict_x(i):
        total = None
        for k in range(5):
            piece = fine[base + 2 * i + k, c0 - 8 : c1 + 8, :] * SPLINE[k]
            total = piece if total is None else total + piece
        r1[i] = dot(ry1[...], stacked2(total))

    repeat(rows1, 1 if rows1 % 19 else 19, restrict_x)
    wide1 = ry1.shape[0]
    high, low = halves(r1[...].reshape(rows1 * wide1, bz))
    l1w[...] = (dot(high, rz1[...]) + dot(low, rz1[...])).reshape(rows1, wide1, hz)
    m0, m1, d0, d1 = margin, margin + hx, hy, 2 * hy
    mid[m0:m1, d0:d1, :] = l1w[2 : 2 + hx, 0:hy, :]
    for i in range(ex):
        total = None
        for k in range(5):
            piece = l1w[2 * i + k] * SPLINE[k]
            total = piece if total is None else total + piece
        l2y[i] = dot(ry2[...], stacked2(total))
    high, low = halves(l2y[...].reshape(ex * ey, hz))
    line2[reach * ex : (reach + 1) * ex] = (dot(high, rz2[...]) + dot(low, rz2[...])).reshape(ex, ey, ez)

    home = line2.at[reach * ex : (reach + 1) * ex]
    lines = both([
        remote(home, line2.at[(reach - d) * ex : (reach - d + 1) * ex], d, 0) for d in (1, -1, 2, -2)
    ])
    rim = both([
        remote(mid.at[m1 - margin : m1, d0:d1], mid.at[0:m0, d0:d1], 1, 0),
        remote(mid.at[m0 : m0 + margin, d0:d1], mid.at[m1 : m1 + margin, d0:d1], -1, 0),
        remote(mid.at[m0:m1, d0:d1], mid.at[m0:m1, 0:d0], 0, 1),
        remote(mid.at[m0:m1, d0:d1], mid.at[m0:m1, d1 : d1 + hy], 0, -1),
    ])
    both(far)
    arrive(lines)
    spot = -low_y
    top[:, spot * ey : (spot + 1) * ey, :] = line2[...]
    fan = both([
        remote(line2, top.at[:, (k * ey) : (k + 1) * ey], 0, -(low_y + k)) for k in range(wy) if low_y + k
    ])
    arrive(rim[:2])
    rim += both([
        remote(mid.at[0:m0, d0:d1], mid.at[0:m0, 0:d0], 0, 1),
        remote(mid.at[m1 : m1 + margin, d0:d1], mid.at[m1 : m1 + margin, 0:d0], 0, 1),
        remote(mid.at[0:m0, d0:d1], mid.at[0:m0, d1 : d1 + hy], 0, -1),
        remote(mid.at[m1 : m1 + margin, d0:d1], mid.at[m1 : m1 + margin, d1 : d1 + hy], 0, -1),
    ])
    arrive(far[:2])
    wide = [(0, x0), (x1, x1 + radius)]
    slim = [(0, x0 - back), (x1 + ahead, x1 + radius)]
    corner = both(
        [remote(fine.at[a:b, c1 - 16 : c1 - 8], fine.at[a:b, 0:8], 0, 1) for a, b in wide]
        + [remote(fine.at[a:b, c1 - 8 : c1], fine.at[a:b, 8:16], 0, 1) for a, b in slim]
        + [remote(fine.at[a:b, c0 + 8 : c0 + 16], fine.at[a:b, c1 + 8 : c1 + 16], 0, -1) for a, b in wide]
        + [remote(fine.at[a:b, c0 : c0 + 8], fine.at[a:b, c1 : c1 + 8], 0, -1) for a, b in slim]
    )

    def correlate_y(ref, source, table, rows, step):
        width = table.shape[0] // terms

        def one(i):
            value = dot(table[...], stacked3(source[i]))
            for member in range(terms):
                ref[member, i] = value[member * width : (member + 1) * width]

        repeat(rows, step, one)

    def correlate_x(ref, source, level, rows, first, step):
        def one(i):
            for member in range(terms):
                total = None
                for position in range(count):
                    piece = source[member, i + first + position] * tap(level, member, position)
                    total = piece if total is None else total + piece
                high, low = halves(total)
                ref[member, 0, i] = high
                ref[member, 1, i] = low

        repeat(rows, step, one)

    def correlate_z(ref, table, a, b):
        size = (b - a) * ref.shape[3]
        total = None
        for member in range(terms):
            high = ref[member, 0, a:b].reshape(size, ref.shape[4])
            low = ref[member, 1, a:b].reshape(size, ref.shape[4])
            piece = dot(high, table[member, 0]) + dot(low, table[member, 0]) + dot(high, table[member, 1])
            total = piece if total is None else total + piece
        return total

    def prolong_x(source, j, first):
        at = j - 2 * first
        if j % 2 == 0:
            c = (j // 2) - first
            return source[c - 1] * 0.125 + source[c] * 0.75 + source[c + 1] * 0.125
        c = (j - 1) // 2 - first
        return source[c] * 0.5 + source[c + 1] * 0.5

    arrive(fan)
    correlate_y(y2, top, ty2, (2 * reach + 1) * ex, 8)
    rows2 = ex + 3
    correlate_x(s2, y2, 2, rows2, reach * ex - 1 - radius, 1)
    tx[...] = correlate_z(s2, tz2, 0, rows2).reshape(tx.shape)
    for j in range(hx + 2):
        ty[j] = dot(uy2[...], stacked2(prolong_x(tx, j - 1, -1)))
    high, low = halves(ty[...].reshape((hx + 2) * ty.shape[1], ez))
    lifted = dot(high, uz2[...]) + dot(low, uz2[...])

    md[...] = lifted.reshape(md.shape)
    arrive(rim[2:])
    correlate_y(y1, mid, ty1, hx + 2 * margin, 2)
    correlate_x(s1, y1, 1, hx + 2, 0, 1)
    md[...] += correlate_z(s1, tz1, 0, hx + 2).reshape(md.shape)
    for j in range(bx):
        high, low = halves(dot(uy1[...], stacked2(prolong_x(md, j, -1))))
        my[0, j] = high
        my[1, j] = low

    arrive(far[2:])
    arrive(corner)
    correlate_y(y0, fine, ty0, bx + 2 * radius, 4)
    correlate_x(s0, y0, 0, bx, 0, 1)
    for a in range(0, bx, 8):
        total = correlate_z(s0, tz0, a, a + 8)
        high = my[0, a : a + 8].reshape(8 * by, hz)
        low = my[1, a : a + 8].reshape(8 * by, hz)
        total = total + dot(high, uz1[...]) + dot(low, uz1[...])
        out[a : a + 8] = total.reshape(8, by, bz)
    for copy in near + far + lines + rim + fan + corner:
        copy.wait_send()


def cyclic_restrict(n):
    rows = np.arange(n)[:, None]
    cols = np.arange(n // 2)[None, :]
    table = np.zeros((n, n // 2), np.float32)
    for k in range(-2, 3):
        table += SPLINE[k + 2] * ((2 * cols + k) % n == rows)
    return table


def body(charges, kernel_taps):
    nx, ny = lax.axis_size("gx"), lax.axis_size("gy")
    levels, terms, count = kernel_taps.shape
    radius = count // 2
    margin = radius + 1
    bx, by, bz = charges.shape
    hx, hy, hz = bx // 2, by // 2, bz // 2
    ex, ey, ez = bx // 4, by // 4, bz // 4
    pad = 16
    wy = min(ny, 5)
    order1 = list(range(hy)) + [-2, -1, hy] + [None] * 5
    ry1 = fixed_table(order1, list(range(-8, by + 8)), len(order1))
    ry2 = fixed_table(list(range(ey)), order1, ey)
    rz1, rz2 = cyclic_restrict(bz), cyclic_restrict(hz)
    wide1 = hy + 8
    wide2 = ey + 8
    uy2 = lifted_table(list(range(-1, hy + 1)), list(range(-1, ey + 2)) + [None] * (wide2 - ey - 3), wide1)
    uy1 = lifted_table(list(range(by)), list(range(-1, hy + 1)) + [None] * (wide1 - hy - 2), by)
    fixed = [twice(ry1), jnp.asarray(rz1, BF16), twice(ry2), jnp.asarray(rz2, BF16), twice(uy2),
             jnp.asarray(rz2.T, BF16), twice(uy1), jnp.asarray(rz1.T, BF16)]
    rows1, rows2 = hx + 3, ex + 3
    vmem = lambda shape, dtype=F32: pltpu.VMEM(shape, dtype)
    scratch = [
        vmem((bx + 2 * radius, by + 2 * pad, bz)),
        vmem((hx + 2 * margin, 3 * hy, hz)),
        vmem((8, 128)),
        vmem((5 * ex, ey, ez)),
        vmem((5 * ex, wy * ey, ez)),
        vmem((terms * by, 3 * (by + 2 * pad)), BF16),
        vmem((terms * wide1, 9 * hy), BF16),
        vmem((terms * wide2, 3 * wy * ey), BF16),
        vmem((terms, 2, bz, bz), BF16),
        vmem((terms, 2, hz, hz), BF16),
        vmem((terms, 2, ez, ez), BF16),
        vmem((terms, bx + 2 * radius, by, bz)),
        vmem((terms, 2, bx, by, bz), BF16),
        vmem((terms, hx + 2 * margin, wide1, hz)),
        vmem((terms, 2, hx + 2, wide1, hz), BF16),
        vmem((terms, 5 * ex, wide2, ez)),
        vmem((terms, 2, rows2, wide2, ez), BF16),
        vmem((8, 128)),
        vmem((rows1, wide1, bz)),
        vmem((rows1, wide1, hz)),
        vmem((8, 128)),
        vmem((ex, ey, hz)),
        vmem((rows2, wide2, ez)),
        vmem((hx + 2, wide1, ez)),
        vmem((hx + 2, wide1, hz)),
        vmem((8, 128)),
        vmem((2, bx, by, hz), BF16),
        pltpu.SemaphoreType.DMA((48,)),
        pltpu.SemaphoreType.DMA((48,)),
    ]
    return pl.pallas_call(
        functools.partial(kernel, nx, ny, radius, terms),
        out_shape=jax.ShapeDtypeStruct(charges.shape, F32),
        in_specs=[pl.BlockSpec(memory_space=pltpu.SMEM)] + [pl.BlockSpec(memory_space=pltpu.VMEM)] * 9,
        out_specs=pl.BlockSpec(memory_space=pltpu.VMEM),
        scratch_shapes=scratch,
        compiler_params=pltpu.CompilerParams(
            collective_id=0, has_side_effects=True, vmem_limit_bytes=60 * 2**20
        ),
    )(kernel_taps.reshape(-1), charges, *fixed)


def solution(mesh):
    return jax.shard_map(
        body,
        mesh=mesh,
        in_specs=(P("gx", "gy", None), P()),
        out_specs=P("gx", "gy", None),
        check_vma=False,
    )
```

```python
import functools

import jax
import jax.numpy as jnp
import numpy as np
from jax import lax
from jax.experimental import pallas as pl
from jax.experimental.pallas import tpu as pltpu
from jax.sharding import PartitionSpec as P

SPLINE = (0.125, 0.5, 0.75, 0.5, 0.125)
F32, BF16 = jnp.float32, jnp.bfloat16
MESH = pl.DeviceIdType.MESH


def spline_at(offset):
    return SPLINE[offset + 2] if -2 <= offset <= 2 else 0.0


def fixed_table(rows, cols, width):
    table = np.zeros((width, len(cols)), np.float32)
    for a, fine in enumerate(rows):
        for b, other in enumerate(cols):
            if fine is not None and other is not None:
                table[a, b] = spline_at(other - 2 * fine)
    return table


def lifted_table(rows, cols, width):
    table = np.zeros((width, len(cols)), np.float32)
    for a, fine in enumerate(rows):
        for b, coarse in enumerate(cols):
            if coarse is not None:
                table[a, b] = spline_at(fine - 2 * coarse)
    return table


def twice(table):
    return jnp.asarray(np.concatenate([table, table], axis=1), BF16)


def halves(value):
    high = value.astype(BF16)
    return high, (value - high.astype(F32)).astype(BF16)


def dot(left, right):
    return jnp.dot(left, right, preferred_element_type=F32)


def stacked2(value):
    high, low = halves(value)
    return jnp.concatenate([high, low], axis=0)


def stacked3(value):
    high, low = halves(value)
    return jnp.concatenate([high, low, high], axis=0)


def repeat(count, step, body):
    def trip(i, carry):
        for k in range(step):
            body(i * step + k)
        return carry

    assert count % step == 0
    lax.fori_loop(0, count // step, trip, 0)


def kernel(nx, ny, radius, terms, taps, q, ry1, rz1, ry2, rz2, uy2, uz2, uy1, uz1, out,
           fine, mid, ext, got, left1, right1, low1, high1, l2w, cols2, seen2, strip2, far2, top,
           ty0, ty1, ty2, tz0, tz1, tz2, y0, s0, y1, s1, y2, s2, r1, l1w, l2y, tx, ty, md, my,
           send, recv):
    bx, by, bz = q.shape
    hx, hy, hz = bx // 2, by // 2, bz // 2
    ex, ey, ez = bx // 4, by // 4, bz // 4
    count = 2 * radius + 1
    margin = radius + 1
    me_x, me_y = lax.axis_index("gx"), lax.axis_index("gy")
    reach = 2
    wy = min(ny, 2 * reach + 1)
    low_y = -((wy - 1) // 2)

    def device(dx, dy):
        return {"gx": lax.rem(me_x + dx + nx, nx), "gy": lax.rem(me_y + dy + ny, ny)}

    peers = {}
    for dx, dy in [(-1, 0), (1, 0), (0, -1), (0, 1), (-2, 0), (2, 0)] + [
        (0, -(low_y + k)) for k in range(wy)
    ]:
        if dx % nx or dy % ny:
            peers[(dx % nx, dy % ny)] = (dx, dy)
    barrier = pltpu.get_barrier_semaphore()
    for dx, dy in peers.values():
        pl.semaphore_signal(barrier, inc=1, device_id=device(dx, dy), device_id_type=MESH)

    def tap(level, member, position):
        return taps[level, member, position]

    def band(level, member, rows, cols, first, cycle, places):
        column = lax.broadcasted_iota(jnp.int32, (rows, cols), 1)
        place = column
        for start, shift in places:
            place = jnp.where(column >= start, column + shift, place)
        offsets = place - lax.broadcasted_iota(jnp.int32, (rows, cols), 0) + first
        if cycle:
            offsets = jnp.where(offsets < 0, offsets + cycle, offsets)
            offsets = jnp.where(offsets >= cycle, offsets - cycle, offsets)
        table = jnp.zeros((rows, cols), F32)
        for position in range(count):
            table = jnp.where(offsets == position, tap(level, member, position), table)
        return table

    def y_table(ref, level, rows, cols, first, cycle, places):
        for member in range(terms):
            high, low = halves(band(level, member, rows, cols, first, cycle, places))
            at = slice(member * rows, (member + 1) * rows)
            ref[at, 0:cols] = high
            ref[at, cols : 2 * cols] = high
            ref[at, 2 * cols : 3 * cols] = low

    def z_table(ref, level, n):
        def rows_of(i):
            start = pl.multiple_of(i * 16, 16)
            offsets = (
                lax.broadcasted_iota(jnp.int32, (16, n), 0)
                + start
                - lax.broadcasted_iota(jnp.int32, (16, n), 1)
                + radius
            )
            offsets = jnp.where(offsets < 0, offsets + n, offsets)
            offsets = jnp.where(offsets >= n, offsets - n, offsets)
            for member in range(terms):
                table = jnp.zeros((16, n), F32)
                for position in range(count):
                    table = jnp.where(offsets == position, tap(level, member, position), table)
                high, low = halves(table)
                ref[member, 0, pl.ds(start, 16), :] = high
                ref[member, 1, pl.ds(start, 16), :] = low

        repeat(n // 16, 1, rows_of)

    sem = [0]

    def remote(source, target, dx, dy):
        index = sem[0]
        sem[0] += 1
        return pltpu.make_async_remote_copy(
            src_ref=source, dst_ref=target, send_sem=send.at[index], recv_sem=recv.at[index],
            device_id=device(dx, dy), device_id_type=MESH,
        )

    def both(copies):
        for copy in copies:
            copy.start()
        return copies

    def arrive(copies):
        for copy in copies:
            copy.wait_recv()

    def weighted(source, i, low, high):
        total = None
        for k in range(-2, 3):
            if low <= 2 * i + k < high:
                piece = source(2 * i + k) * SPLINE[k + 2]
                total = piece if total is None else total + piece
        return total

    rows1, rows2 = hx + 2, ex + 3
    wide1, wide2 = ry1.shape[0], ry2.shape[0]
    for i in range(rows1):
        r1[i] = dot(ry1[...], stacked2(weighted(lambda f: q[f], i - 1, 0, bx)))
    high, low = halves(r1[...].reshape(rows1 * wide1, bz))
    l1w[...] = (dot(high, rz1[...]) + dot(low, rz1[...])).reshape(rows1, wide1, hz)
    for i in range(rows2):
        l2y[i] = dot(ry2[...], stacked2(weighted(lambda f: l1w[f + 1], i - 1, -1, hx + 1)))
    high, low = halves(l2y[...].reshape(rows2 * wide2, hz))
    l2w[...] = (dot(high, rz2[...]) + dot(low, rz2[...])).reshape(rows2, wide2, ez)
    x0, x1 = radius, radius + bx
    extra = radius - 8
    per = 8 // extra
    for i in range(bx):
        g, r = i // per, extra * (i % per)
        ext[0, g, r : r + extra] = q[i, by - radius : by - 8]
        ext[1, g, r : r + extra] = q[i, 8:radius]

    pl.semaphore_wait(barrier, len(peers))
    spot = -low_y
    fan = both([
        remote(l2w, cols2.at[k], 0, -(low_y + k)) for k in range(wy) if low_y + k
    ])
    rim = both([
        remote(l1w.at[rows1 - margin - 1 : rows1], low1, 1, 0),
        remote(l1w.at[0 : margin + 1], high1, -1, 0),
    ])
    g1 = bx // per
    side = both([
        remote(q.at[:, by - 8 : by], fine.at[x0:x1, by : by + 8], 0, 1),
        remote(q.at[:, 0:8], fine.at[x0:x1, by + 8 : by + 16], 0, -1),
        remote(ext.at[0, 0:g1], got.at[0, 0:g1], 0, 1),
        remote(ext.at[1, 0:g1], got.at[1, 0:g1], 0, -1),
    ])
    y_table(ty2, 2, wide2, wy * ey, low_y * ey + 1 + radius, wy * ey if ny <= 2 * reach + 1 else 0, [])
    z_table(tz2, 2, ez)

    cols2[spot] = l2w[...]
    arrive(fan)
    for k in range(wy):
        strip2[:, k * ey : (k + 1) * ey, :] = cols2[k, :, 0:ey, :]
    for k in range(wy):
        for at, place in ((ey, (k + 1) * ey), (ey + 1, (k + 1) * ey + 1), (ey + 2, k * ey - 1)):
            if ny <= 2 * reach + 1:
                place %= wy * ey
            if 0 <= place < wy * ey:
                strip2[:, place : place + 1, :] += cols2[k, :, at : at + 1, :]
    tail = margin - ex + 2
    lines = both([
        remote(strip2, seen2.at[0], 1, 0),
        remote(strip2, seen2.at[1], -1, 0),
        remote(strip2.at[rows2 - tail : rows2], far2.at[0], 2, 0),
        remote(strip2.at[0:tail], far2.at[1], -2, 0),
    ])
    far = both([
        remote(q.at[bx - radius : bx], fine.at[0:x0, 0:by], 1, 0),
        remote(q.at[0:radius], fine.at[x1 : x1 + radius, 0:by], -1, 0),
    ])
    z_table(tz1, 1, hz)

    arrive(rim)
    mid[0 : margin + 1, 0:wide1] = low1[...]
    mid[margin + 1 : margin + hx - 1, 0:wide1] = l1w[2:hx]
    mid[margin + hx - 1 : margin + hx + margin, 0:wide1] = high1[...]
    for i, j in ((margin - 1, 0), (margin, 1), (margin + hx - 1, hx), (margin + hx, hx + 1)):
        mid[i, 0:wide1] += l1w[j]
    left1[...] = mid[:, 1 : hy + 1, :]
    right1[:, 0:1, :] = mid[:, hy + 1 : hy + 2, :]
    right1[:, 1:hy, :] = mid[:, 0 : hy - 1, :]
    rim2 = both([
        remote(left1, mid.at[:, wide1 : wide1 + hy], 0, 1),
        remote(right1, mid.at[:, wide1 + hy : wide1 + 2 * hy], 0, -1),
    ])
    fine[x0:x1, 0:by, :] = q[...]
    y_table(ty0, 0, by, by + 24, radius, 0, [(by, -by - 8), (by + 8, -8), (by + 16, -by - 16 - radius), (by + 16 + extra, -8 - extra), (by + 16 + 2 * extra, 1000)])
    y_table(ty1, 1, wide1, wide1 + 2 * hy, radius + 1, 0, [(hy + 1, -hy - 2), (hy + 2, 1000), (wide1, -wide1 - hy + 1), (wide1 + hy, -wide1 - 1)])
    z_table(tz0, 0, bz)
    spare = jnp.zeros((8 - 2 * extra, bz), F32)

    def unpack(rows, first):
        for n, i in enumerate(rows):
            g, r = first + n // per, extra * (n % per)
            fine[i, by + 16 : by + 16 + extra] = got[0, g, r : r + extra]
            fine[i, by + 16 + extra : by + 16 + 2 * extra] = got[1, g, r : r + extra]
            fine[i, by + 16 + 2 * extra : by + 24] = spare

    outer = list(range(x0)) + list(range(x1, x1 + radius))
    arrive(far)
    for n, i in enumerate(outer):
        g, r = g1 + n // per, extra * (n % per)
        ext[0, g, r : r + extra] = fine[i, by - radius : by - 8, :]
        ext[1, g, r : r + extra] = fine[i, 8:radius, :]
    g2 = ext.shape[1]
    corner = both(
        [remote(fine.at[a:b, by - 8 : by], fine.at[a:b, by : by + 8], 0, 1) for a, b in ((0, x0), (x1, x1 + radius))]
        + [remote(fine.at[a:b, 0:8], fine.at[a:b, by + 8 : by + 16], 0, -1) for a, b in ((0, x0), (x1, x1 + radius))]
        + [remote(ext.at[0, g1:g2], got.at[0, g1:g2], 0, 1), remote(ext.at[1, g1:g2], got.at[1, g1:g2], 0, -1)]
    )

    def correlate_y(ref, source, table, rows, step, first=0):
        width = table.shape[0] // terms

        def one(i):
            i = i + first
            value = dot(table[...], stacked3(source[i]))
            for member in range(terms):
                ref[member, i] = value[member * width : (member + 1) * width]

        repeat(rows, step, one)

    def correlate_x(ref, source, level, rows, first, step):
        def one(i):
            for member in range(terms):
                total = None
                for position in range(count):
                    piece = source[member, i + first + position] * tap(level, member, position)
                    total = piece if total is None else total + piece
                high, low = halves(total)
                ref[member, 0, i] = high
                ref[member, 1, i] = low

        repeat(rows, step, one)

    def correlate_z(ref, table, a, b):
        size = (b - a) * ref.shape[3]
        total = None
        for member in range(terms):
            high = ref[member, 0, a:b].reshape(size, ref.shape[4])
            low = ref[member, 1, a:b].reshape(size, ref.shape[4])
            piece = dot(high, table[member, 0]) + dot(low, table[member, 0]) + dot(high, table[member, 1])
            total = piece if total is None else total + piece
        return total

    def prolong_x(source, j, first):
        at = j - 2 * first
        if j % 2 == 0:
            c = (j // 2) - first
            return source[c - 1] * 0.125 + source[c] * 0.75 + source[c + 1] * 0.125
        c = (j - 1) // 2 - first
        return source[c] * 0.5 + source[c + 1] * 0.5

    arrive(side)
    unpack(range(x0, x1), 0)
    correlate_y(y0, fine, ty0, bx, 4, x0)

    arrive(lines)
    top[...] = jnp.zeros(top.shape, F32)
    home = radius
    for first, source in ((home, strip2), (home - ex, seen2.at[0]), (home + ex, seen2.at[1])):
        top[first : first + rows2] += source[...]
    top[0:tail] += far2[0]
    top[home + 2 * ex : home + 2 * ex + tail] += far2[1]
    correlate_y(y2, top, ty2, top.shape[0], top.shape[0])
    correlate_x(s2, y2, 2, rows2, 0, 1)
    tx[...] = correlate_z(s2, tz2, 0, rows2).reshape(tx.shape)
    for j in range(hx + 2):
        ty[j] = dot(uy2[...], stacked2(prolong_x(tx, j - 1, -1)))
    high, low = halves(ty[...].reshape((hx + 2) * ty.shape[1], ez))
    lifted = dot(high, uz2[...]) + dot(low, uz2[...])

    md[...] = lifted.reshape(md.shape)
    arrive(rim2)
    correlate_y(y1, mid, ty1, hx + 2 * margin, 2)
    correlate_x(s1, y1, 1, hx + 2, 0, 1)
    md[...] += correlate_z(s1, tz1, 0, hx + 2).reshape(md.shape)
    for j in range(bx):
        high, low = halves(dot(uy1[...], stacked2(prolong_x(md, j, -1))))
        my[0, j] = high
        my[1, j] = low

    arrive(corner)
    unpack(outer, g1)
    correlate_y(y0, fine, ty0, x0, 5)
    correlate_y(y0, fine, ty0, radius, 5, x1)
    correlate_x(s0, y0, 0, bx, 0, 1)
    for a in range(0, bx, 8):
        total = correlate_z(s0, tz0, a, a + 8)
        high = my[0, a : a + 8].reshape(8 * by, hz)
        low = my[1, a : a + 8].reshape(8 * by, hz)
        total = total + dot(high, uz1[...]) + dot(low, uz1[...])
        out[a : a + 8] = total.reshape(8, by, bz)
    for copy in fan + rim + side + lines + far + rim2 + corner:
        copy.wait_send()


def cyclic_restrict(n):
    rows = np.arange(n)[:, None]
    cols = np.arange(n // 2)[None, :]
    table = np.zeros((n, n // 2), np.float32)
    for k in range(-2, 3):
        table += SPLINE[k + 2] * ((2 * cols + k) % n == rows)
    return table


def body(charges, kernel_taps):
    nx, ny = lax.axis_size("gx"), lax.axis_size("gy")
    levels, terms, count = kernel_taps.shape
    radius = count // 2
    margin = radius + 1
    bx, by, bz = charges.shape
    hx, hy, hz = bx // 2, by // 2, bz // 2
    ex, ey, ez = bx // 4, by // 4, bz // 4
    pad = 16
    wy = min(ny, 5)
    order1 = list(range(hy)) + [hy, -1] + [None] * 6
    ry1 = fixed_table(order1, list(range(by)), len(order1))
    order2 = list(range(ey)) + [ey, ey + 1, -1] + [None] * 5
    ry2 = fixed_table(order2, order1, len(order2))
    rz1, rz2 = cyclic_restrict(bz), cyclic_restrict(hz)
    wide1 = hy + 8
    wide2 = ey + 8
    uy2 = lifted_table(list(range(-1, hy + 1)), list(range(-1, ey + 2)) + [None] * (wide2 - ey - 3), wide1)
    uy1 = lifted_table(list(range(by)), list(range(-1, hy + 1)) + [None] * (wide1 - hy - 2), by)
    fixed = [twice(ry1), jnp.asarray(rz1, BF16), twice(ry2), jnp.asarray(rz2, BF16), twice(uy2),
             jnp.asarray(rz2.T, BF16), twice(uy1), jnp.asarray(rz1.T, BF16)]
    rows1, rows2 = hx + 2, ex + 3
    extra = radius - 8
    packed = -(-(bx + 2 * radius) * extra // 8)
    scratch = [
        pltpu.VMEM(shape, dtype)
        for shape, dtype in (
            ((bx + 2 * radius, by + 24, bz), F32),
            ((hx + 2 * margin, wide1 + 2 * hy, hz), F32),
            ((2, packed, 8, bz), F32),
            ((2, packed, 8, bz), F32),
            ((hx + 2 * margin, hy, hz), F32),
            ((hx + 2 * margin, hy, hz), F32),
            ((margin + 1, wide1, hz), F32),
            ((margin + 1, wide1, hz), F32),
            ((rows2, wide2, ez), F32),
            ((wy, rows2, wide2, ez), F32),
            ((2, rows2, wy * ey, ez), F32),
            ((rows2, wy * ey, ez), F32),
            ((2, margin - ex + 2, wy * ey, ez), F32),
            ((rows2 + 2 * radius, wy * ey, ez), F32),
            ((terms * by, 3 * (by + 24)), BF16),
            ((terms * wide1, 3 * (wide1 + 2 * hy)), BF16),
            ((terms * wide2, 3 * wy * ey), BF16),
            ((terms, 2, bz, bz), BF16),
            ((terms, 2, hz, hz), BF16),
            ((terms, 2, ez, ez), BF16),
            ((terms, bx + 2 * radius, by, bz), F32),
            ((terms, 2, bx, by, bz), BF16),
            ((terms, hx + 2 * margin, wide1, hz), F32),
            ((terms, 2, hx + 2, wide1, hz), BF16),
            ((terms, rows2 + 2 * radius, wide2, ez), F32),
            ((terms, 2, rows2, wide2, ez), BF16),
            ((rows1, wide1, bz), F32),
            ((rows1, wide1, hz), F32),
            ((rows2, wide2, hz), F32),
            ((rows2, wide2, ez), F32),
            ((hx + 2, wide1, ez), F32),
            ((hx + 2, wide1, hz), F32),
            ((2, bx, by, hz), BF16),
        )
    ] + [
        pltpu.SemaphoreType.DMA((48,)),
        pltpu.SemaphoreType.DMA((48,)),
    ]
    return pl.pallas_call(
        functools.partial(kernel, nx, ny, radius, terms),
        out_shape=jax.ShapeDtypeStruct(charges.shape, F32),
        in_specs=[pl.BlockSpec(memory_space=pltpu.SMEM)] + [pl.BlockSpec(memory_space=pltpu.VMEM)] * 9,
        out_specs=pl.BlockSpec(memory_space=pltpu.VMEM),
        scratch_shapes=scratch,
        compiler_params=pltpu.CompilerParams(
            collective_id=0, has_side_effects=True, vmem_limit_bytes=60 * 2**20
        ),
    )(kernel_taps, charges, *fixed)


def solution(mesh):
    return jax.shard_map(
        body,
        mesh=mesh,
        in_specs=(P("gx", "gy", None), P()),
        out_specs=P("gx", "gy", None),
        check_vma=False,
    )
```

```python
import functools

import jax
import jax.numpy as jnp
import numpy as np
from jax import lax
from jax.experimental import pallas as pl
from jax.experimental.pallas import tpu as pltpu
from jax.sharding import PartitionSpec as P

SPLINE = (0.125, 0.5, 0.75, 0.5, 0.125)
F32, BF16 = jnp.float32, jnp.bfloat16
MESH = pl.DeviceIdType.MESH


def spline_at(offset):
    return SPLINE[offset + 2] if -2 <= offset <= 2 else 0.0


def fixed_table(rows, cols, width):
    table = np.zeros((width, len(cols)), np.float32)
    for a, fine in enumerate(rows):
        for b, other in enumerate(cols):
            if fine is not None and other is not None:
                table[a, b] = spline_at(other - 2 * fine)
    return table


def lifted_table(rows, cols, width):
    table = np.zeros((width, len(cols)), np.float32)
    for a, fine in enumerate(rows):
        for b, coarse in enumerate(cols):
            if coarse is not None:
                table[a, b] = spline_at(fine - 2 * coarse)
    return table


def twice(table):
    return jnp.asarray(np.concatenate([table, table], axis=1), BF16)


def halves(value):
    high = value.astype(BF16)
    return high, (value - high.astype(F32)).astype(BF16)


def dot(left, right):
    return jnp.dot(left, right, preferred_element_type=F32)


def stacked2(value):
    high, low = halves(value)
    return jnp.concatenate([high, low], axis=0)


def stacked3(value):
    high, low = halves(value)
    return jnp.concatenate([high, low, high], axis=0)


def repeat(count, step, body):
    def trip(i, carry):
        for k in range(step):
            body(i * step + k)
        return carry

    assert count % step == 0
    lax.fori_loop(0, count // step, trip, 0)


def kernel(nx, ny, radius, terms, taps, q, ry1, rz1, ry2, rz2, uy2, uz2, uy1, uz1, out,
           fine, mid, ext, got, left1, right1, low1, high1, l2w, cols2, seen2, strip2, far2, top,
           ty0, ty1, ty2, tz0, tz1, tz2, y0, s0, y1, s1, y2, s2, r1, l1w, l2y, tx, ty, md, my,
           send, recv):
    bx, by, bz = q.shape
    hx, hy, hz = bx // 2, by // 2, bz // 2
    ex, ey, ez = bx // 4, by // 4, bz // 4
    count = 2 * radius + 1
    margin = radius + 1
    me_x, me_y = lax.axis_index("gx"), lax.axis_index("gy")
    reach = 2
    wy = min(ny, 2 * reach + 1)
    low_y = -((wy - 1) // 2)

    def device(dx, dy):
        return {"gx": lax.rem(me_x + dx + nx, nx), "gy": lax.rem(me_y + dy + ny, ny)}

    peers = {}
    for dx, dy in [(-1, 0), (1, 0), (0, -1), (0, 1), (-2, 0), (2, 0)] + [
        (0, -(low_y + k)) for k in range(wy)
    ]:
        if dx % nx or dy % ny:
            peers[(dx % nx, dy % ny)] = (dx, dy)
    barrier = pltpu.get_barrier_semaphore()
    for dx, dy in peers.values():
        pl.semaphore_signal(barrier, inc=1, device_id=device(dx, dy), device_id_type=MESH)

    def tap(level, member, position):
        return taps[level, member, position]

    def band(level, member, rows, cols, first, cycle, places):
        column = lax.broadcasted_iota(jnp.int32, (rows, cols), 1)
        place = column
        for start, shift in places:
            place = jnp.where(column >= start, column + shift, place)
        offsets = place - lax.broadcasted_iota(jnp.int32, (rows, cols), 0) + first
        if cycle:
            offsets = jnp.where(offsets < 0, offsets + cycle, offsets)
            offsets = jnp.where(offsets >= cycle, offsets - cycle, offsets)
        table = jnp.zeros((rows, cols), F32)
        for position in range(count):
            table = jnp.where(offsets == position, tap(level, member, position), table)
        return table

    def y_table(ref, level, rows, cols, first, cycle, places):
        for member in range(terms):
            high, low = halves(band(level, member, rows, cols, first, cycle, places))
            at = slice(member * rows, (member + 1) * rows)
            ref[at, 0:cols] = high
            ref[at, cols : 2 * cols] = high
            ref[at, 2 * cols : 3 * cols] = low

    def z_table(ref, level, n):
        def rows_of(i):
            start = pl.multiple_of(i * 16, 16)
            offsets = (
                lax.broadcasted_iota(jnp.int32, (16, n), 0)
                + start
                - lax.broadcasted_iota(jnp.int32, (16, n), 1)
                + radius
            )
            offsets = jnp.where(offsets < 0, offsets + n, offsets)
            offsets = jnp.where(offsets >= n, offsets - n, offsets)
            for member in range(terms):
                table = jnp.zeros((16, n), F32)
                for position in range(count):
                    table = jnp.where(offsets == position, tap(level, member, position), table)
                high, low = halves(table)
                ref[0, pl.ds(pl.multiple_of(member * n + start, 16), 16), :] = high
                ref[1, pl.ds(pl.multiple_of(member * n + start, 16), 16), :] = low

        repeat(n // 16, 1, rows_of)

    sem = [0]

    def remote(source, target, dx, dy):
        index = sem[0]
        sem[0] += 1
        return pltpu.make_async_remote_copy(
            src_ref=source, dst_ref=target, send_sem=send.at[index], recv_sem=recv.at[index],
            device_id=device(dx, dy), device_id_type=MESH,
        )

    def both(copies):
        for copy in copies:
            copy.start()
        return copies

    def arrive(copies):
        for copy in copies:
            copy.wait_recv()

    x0, x1 = radius, radius + bx
    extra = radius - 8
    per = 8 // extra
    def weighted(source, i, low, high):
        total = None
        for k in range(-2, 3):
            if low <= 2 * i + k < high:
                piece = source(2 * i + k) * SPLINE[k + 2]
                total = piece if total is None else total + piece
        return total

    rows1, rows2 = hx + 2, ex + 3
    wide1, wide2 = ry1.shape[0], ry2.shape[0]
    for i in range(rows1):
        r1[i] = dot(ry1[...], stacked2(weighted(lambda f: q[f], i - 1, 0, bx)))
    high, low = halves(r1[...].reshape(rows1 * wide1, bz))
    l1w[...] = (dot(high, rz1[...]) + dot(low, rz1[...])).reshape(rows1, wide1, hz)
    for i in range(rows2):
        l2y[i] = dot(ry2[...], stacked2(weighted(lambda f: l1w[f + 1], i - 1, -1, hx + 1)))
    high, low = halves(l2y[...].reshape(rows2 * wide2, hz))
    l2w[...] = (dot(high, rz2[...]) + dot(low, rz2[...])).reshape(rows2, wide2, ez)
    pl.semaphore_wait(barrier, len(peers))
    spot = -low_y
    fan = both([
        remote(l2w, cols2.at[k], 0, -(low_y + k)) for k in range(wy) if low_y + k
    ])
    rim = both([
        remote(l1w.at[rows1 - margin - 1 : rows1], low1, 1, 0),
        remote(l1w.at[0 : margin + 1], high1, -1, 0),
    ])
    g1 = bx // per
    side = both([
        remote(q.at[:, by - 8 : by], fine.at[x0:x1, by : by + 8], 0, 1),
        remote(q.at[:, 0:8], fine.at[x0:x1, by + 8 : by + 16], 0, -1),
    ])
    for i in range(bx):
        g, r = i // per, extra * (i % per)
        ext[0, g, r : r + extra] = q[i, by - radius : by - 8]
        ext[1, g, r : r + extra] = q[i, 8:radius]

    side += both([
        remote(ext.at[0, 0:g1], got.at[0, 0:g1], 0, 1),
        remote(ext.at[1, 0:g1], got.at[1, 0:g1], 0, -1),
    ])
    y_table(ty2, 2, wide2, wy * ey, low_y * ey + 1 + radius, wy * ey if ny <= 2 * reach + 1 else 0, [])
    z_table(tz2, 2, ez)

    cols2[spot] = l2w[...]
    arrive(fan)
    for k in range(wy):
        strip2[:, k * ey : (k + 1) * ey, :] = cols2[k, :, 0:ey, :]
    for k in range(wy):
        for at, place in ((ey, (k + 1) * ey), (ey + 1, (k + 1) * ey + 1), (ey + 2, k * ey - 1)):
            if ny <= 2 * reach + 1:
                place %= wy * ey
            if 0 <= place < wy * ey:
                strip2[:, place : place + 1, :] += cols2[k, :, at : at + 1, :]
    tail = margin - ex + 2
    lines = both([
        remote(strip2, seen2.at[0], 1, 0),
        remote(strip2, seen2.at[1], -1, 0),
        remote(strip2.at[rows2 - tail : rows2], far2.at[0], 2, 0),
        remote(strip2.at[0:tail], far2.at[1], -2, 0),
    ])
    far = both([
        remote(q.at[bx - radius : bx], fine.at[0:x0, 0:by], 1, 0),
        remote(q.at[0:radius], fine.at[x1 : x1 + radius, 0:by], -1, 0),
    ])
    fine[x0:x1, 0:by, :] = q[...]
    y_table(ty0, 0, by, by + 24, radius, 0, [(by, -by - 8), (by + 8, -8), (by + 16, -by - 16 - radius), (by + 16 + extra, -8 - extra), (by + 16 + 2 * extra, 1000)])
    y_table(ty1, 1, wide1, wide1 + 2 * hy, radius + 1, 0, [(hy + 1, -hy - 2), (hy + 2, 1000), (wide1, -wide1 - hy + 1), (wide1 + hy, -wide1 - 1)])
    z_table(tz0, 0, bz)
    spare = jnp.zeros((8 - 2 * extra, bz), F32)

    def unpack(rows, first):
        for n, i in enumerate(rows):
            g, r = first + n // per, extra * (n % per)
            fine[i, by + 16 : by + 16 + extra] = got[0, g, r : r + extra]
            fine[i, by + 16 + extra : by + 16 + 2 * extra] = got[1, g, r : r + extra]
            fine[i, by + 16 + 2 * extra : by + 24] = spare

    z_table(tz1, 1, hz)

    arrive(rim)
    mid[0 : margin + 1, 0:wide1] = low1[...]
    mid[margin + 1 : margin + hx - 1, 0:wide1] = l1w[2:hx]
    mid[margin + hx - 1 : margin + hx + margin, 0:wide1] = high1[...]
    for i, j in ((margin - 1, 0), (margin, 1), (margin + hx - 1, hx), (margin + hx, hx + 1)):
        mid[i, 0:wide1] += l1w[j]
    left1[...] = mid[:, 1 : hy + 1, :]
    right1[:, 0:1, :] = mid[:, hy + 1 : hy + 2, :]
    right1[:, 1:hy, :] = mid[:, 0 : hy - 1, :]
    rim2 = both([
        remote(left1, mid.at[:, wide1 : wide1 + hy], 0, 1),
        remote(right1, mid.at[:, wide1 + hy : wide1 + 2 * hy], 0, -1),
    ])
    outer = list(range(x0)) + list(range(x1, x1 + radius))
    def correlate_y(ref, source, table, rows, step, first=0):
        width = table.shape[0] // terms

        def one(i):
            i = i + first
            value = dot(table[...], stacked3(source[i]))
            for member in range(terms):
                ref[member, i] = value[member * width : (member + 1) * width]

        repeat(rows, step, one)

    def correlate_x(ref, source, level, rows, first, step, start=0):
        def one(i):
            i = i + start
            for member in range(terms):
                total = None
                for position in range(count):
                    piece = source[member, i + first + position] * tap(level, member, position)
                    total = piece if total is None else total + piece
                high, low = halves(total)
                at = slice(member * total.shape[1], (member + 1) * total.shape[1])
                ref[0, i, :, at] = high
                ref[1, i, :, at] = low

        repeat(rows, step, one)

    def correlate_z(ref, table, a, b):
        size = (b - a) * ref.shape[2]
        high = ref[0, a:b].reshape(size, ref.shape[3])
        low = ref[1, a:b].reshape(size, ref.shape[3])
        return dot(high, table[0]) + dot(low, table[0]) + dot(high, table[1])

    def prolong_x(source, j, first):
        at = j - 2 * first
        if j % 2 == 0:
            c = (j // 2) - first
            return source[c - 1] * 0.125 + source[c] * 0.75 + source[c + 1] * 0.125
        c = (j - 1) // 2 - first
        return source[c] * 0.5 + source[c + 1] * 0.5

    arrive(side)
    unpack(range(x0, x1), 0)
    correlate_y(y0, fine, ty0, bx, 4, x0)

    arrive(lines)
    top[...] = jnp.zeros(top.shape, F32)
    home = radius
    for first, source in ((home, strip2), (home - ex, seen2.at[0]), (home + ex, seen2.at[1])):
        top[first : first + rows2] += source[...]
    top[0:tail] += far2[0]
    top[home + 2 * ex : home + 2 * ex + tail] += far2[1]
    correlate_y(y2, top, ty2, top.shape[0], top.shape[0])
    correlate_x(s2, y2, 2, rows2, 0, 1)
    tx[...] = correlate_z(s2, tz2, 0, rows2).reshape(tx.shape)
    for j in range(hx + 2):
        ty[j] = dot(uy2[...], stacked2(prolong_x(tx, j - 1, -1)))
    high, low = halves(ty[...].reshape((hx + 2) * ty.shape[1], ez))
    lifted = dot(high, uz2[...]) + dot(low, uz2[...])

    md[...] = lifted.reshape(md.shape)
    arrive(rim2)
    correlate_y(y1, mid, ty1, hx + 2 * margin, 2)
    correlate_x(s1, y1, 1, hx + 2, 0, 1)
    md[...] += correlate_z(s1, tz1, 0, hx + 2).reshape(md.shape)
    for j in range(bx):
        high, low = halves(dot(uy1[...], stacked2(prolong_x(md, j, -1))))
        my[0, j] = high
        my[1, j] = low

    def finish(a, b):
        high = my[0, a:b].reshape((b - a) * by, hz)
        low = my[1, a:b].reshape((b - a) * by, hz)
        total = correlate_z(s0, tz0, a, b) + dot(high, uz1[...]) + dot(low, uz1[...])
        out[a:b] = total.reshape(b - a, by, bz)

    correlate_x(s0, y0, 0, bx - 2 * radius, 0, 1, radius)
    finish(radius, bx - radius)
    arrive(far)
    for n, i in enumerate(outer):
        g, r = g1 + n // per, extra * (n % per)
        ext[0, g, r : r + extra] = fine[i, by - radius : by - 8, :]
        ext[1, g, r : r + extra] = fine[i, 8:radius, :]
    g2 = ext.shape[1]
    corner = both(
        [remote(fine.at[a:b, by - 8 : by], fine.at[a:b, by : by + 8], 0, 1) for a, b in ((0, x0), (x1, x1 + radius))]
        + [remote(fine.at[a:b, 0:8], fine.at[a:b, by + 8 : by + 16], 0, -1) for a, b in ((0, x0), (x1, x1 + radius))]
        + [remote(ext.at[0, g1:g2], got.at[0, g1:g2], 0, 1), remote(ext.at[1, g1:g2], got.at[1, g1:g2], 0, -1)]
    )

    arrive(corner)
    unpack(outer, g1)
    correlate_y(y0, fine, ty0, x0, 5)
    correlate_y(y0, fine, ty0, radius, 5, x1)
    correlate_x(s0, y0, 0, radius, 0, 1)
    correlate_x(s0, y0, 0, radius, 0, 1, bx - radius)
    finish(0, radius)
    finish(bx - radius, bx)
    for copy in fan + rim + side + lines + far + rim2 + corner:
        copy.wait_send()


def cyclic_restrict(n):
    rows = np.arange(n)[:, None]
    cols = np.arange(n // 2)[None, :]
    table = np.zeros((n, n // 2), np.float32)
    for k in range(-2, 3):
        table += SPLINE[k + 2] * ((2 * cols + k) % n == rows)
    return table


def body(charges, kernel_taps):
    nx, ny = lax.axis_size("gx"), lax.axis_size("gy")
    levels, terms, count = kernel_taps.shape
    radius = count // 2
    margin = radius + 1
    bx, by, bz = charges.shape
    hx, hy, hz = bx // 2, by // 2, bz // 2
    ex, ey, ez = bx // 4, by // 4, bz // 4
    pad = 16
    wy = min(ny, 5)
    order1 = list(range(hy)) + [hy, -1] + [None] * 6
    ry1 = fixed_table(order1, list(range(by)), len(order1))
    order2 = list(range(ey)) + [ey, ey + 1, -1] + [None] * 5
    ry2 = fixed_table(order2, order1, len(order2))
    rz1, rz2 = cyclic_restrict(bz), cyclic_restrict(hz)
    wide1 = hy + 8
    wide2 = ey + 8
    uy2 = lifted_table(list(range(-1, hy + 1)), list(range(-1, ey + 2)) + [None] * (wide2 - ey - 3), wide1)
    uy1 = lifted_table(list(range(by)), list(range(-1, hy + 1)) + [None] * (wide1 - hy - 2), by)
    fixed = [twice(ry1), jnp.asarray(rz1, BF16), twice(ry2), jnp.asarray(rz2, BF16), twice(uy2),
             jnp.asarray(rz2.T, BF16), twice(uy1), jnp.asarray(rz1.T, BF16)]
    rows1, rows2 = hx + 2, ex + 3
    extra = radius - 8
    packed = -(-(bx + 2 * radius) * extra // 8)
    scratch = [
        pltpu.VMEM(shape, dtype)
        for shape, dtype in (
            ((bx + 2 * radius, by + 24, bz), F32),
            ((hx + 2 * margin, wide1 + 2 * hy, hz), F32),
            ((2, packed, 8, bz), F32),
            ((2, packed, 8, bz), F32),
            ((hx + 2 * margin, hy, hz), F32),
            ((hx + 2 * margin, hy, hz), F32),
            ((margin + 1, wide1, hz), F32),
            ((margin + 1, wide1, hz), F32),
            ((rows2, wide2, ez), F32),
            ((wy, rows2, wide2, ez), F32),
            ((2, rows2, wy * ey, ez), F32),
            ((rows2, wy * ey, ez), F32),
            ((2, margin - ex + 2, wy * ey, ez), F32),
            ((rows2 + 2 * radius, wy * ey, ez), F32),
            ((terms * by, 3 * (by + 24)), BF16),
            ((terms * wide1, 3 * (wide1 + 2 * hy)), BF16),
            ((terms * wide2, 3 * wy * ey), BF16),
            ((2, terms * bz, bz), BF16),
            ((2, terms * hz, hz), BF16),
            ((2, terms * ez, ez), BF16),
            ((terms, bx + 2 * radius, by, bz), F32),
            ((2, bx, by, terms * bz), BF16),
            ((terms, hx + 2 * margin, wide1, hz), F32),
            ((2, hx + 2, wide1, terms * hz), BF16),
            ((terms, rows2 + 2 * radius, wide2, ez), F32),
            ((2, rows2, wide2, terms * ez), BF16),
            ((rows1, wide1, bz), F32),
            ((rows1, wide1, hz), F32),
            ((rows2, wide2, hz), F32),
            ((rows2, wide2, ez), F32),
            ((hx + 2, wide1, ez), F32),
            ((hx + 2, wide1, hz), F32),
            ((2, bx, by, hz), BF16),
        )
    ] + [
        pltpu.SemaphoreType.DMA((48,)),
        pltpu.SemaphoreType.DMA((48,)),
    ]
    return pl.pallas_call(
        functools.partial(kernel, nx, ny, radius, terms),
        out_shape=jax.ShapeDtypeStruct(charges.shape, F32),
        in_specs=[pl.BlockSpec(memory_space=pltpu.SMEM)] + [pl.BlockSpec(memory_space=pltpu.VMEM)] * 9,
        out_specs=pl.BlockSpec(memory_space=pltpu.VMEM),
        scratch_shapes=scratch,
        compiler_params=pltpu.CompilerParams(
            collective_id=0, has_side_effects=True, vmem_limit_bytes=60 * 2**20
        ),
    )(kernel_taps, charges, *fixed)


def solution(mesh):
    return jax.shard_map(
        body,
        mesh=mesh,
        in_specs=(P("gx", "gy", None), P()),
        out_specs=P("gx", "gy", None),
        check_vma=False,
    )
```
